256 devices in a mesh: band: 64 (over x, z, core), rep: 4 (over y).
Axes of the slice: x: 4, y: 4, z: 8, core: 2. Of those that a mesh axis runs over, the one named last changes fastest.
Arguments:
- patches: bfloat16 [8, 4, 80, 64, 768], P('rep', None, None, 'band'), may hold values from -6 to 6
- variable_group_index: int32 [5], replicated, may hold values from 0 to 2, as said below
- frozen_patch_weight: bfloat16 [3, 16, 512], replicated, may hold values from -0.625 to 0.625
- adapter_down: bfloat16 [80, 16], P('rep'), may hold values from -0.625 to 0.625
- adapter_up: bfloat16 [16, 512], P(None, 'rep'), may hold values from -1.5 to 1.5
- level_merge_weight: bfloat16 [4, 512, 512], replicated, may hold values from -0.125 to 0.125
- window_patch_mixer: bfloat16 [96, 96], replicated, may hold values from -0.625 to 0.625
- column_block_owner: int32 [64], replicated, may hold values from 0 to 63, each once
- mixed_token_gradient: bfloat16 [8, 64, 64, 12, 512], P('rep', 'band'), may hold values from -0.01171875 to 0.01171875
Outputs:
- mixed: bfloat16 [8, 64, 64, 12, 512], P('rep', 'band')
- first_factor_gradient: float32 [80, 16], P('rep')
- second_factor_gradient: float32 [16, 512], P(None, 'rep')
The draws below stay inside these ranges and needn't reach their ends.
Inputs may be any that keep to these rules, and one draw needn't show every extreme that they name: Column block j goes to the band device column_block_owner[j]; each device owns one block. `variable_group_index`: every one of the 3 groups holds at least one variable.
All inputs are finite; a program needn't handle non-finite values.
Results may differ from the reference program's by a relative error of at most 0.01.
Values may be sent and summed in bfloat16 or wider, within the bound.
A program may use at most 128 MiB of HBM per device.

```python
import jax
import jax.numpy as jnp
from jax import lax

EMBED_WIDTH = 512
VARS = 5
PIX = 16
LEV = 4
ADAPTER_RANK = 16
G = 3
WLAT = 8
WLON = 12
COLS = 768
LEVEL_CHANNELS = 80
WT = 96
LAT = 64
BLOCKS = 64
BW = 12
NS = 8
N_BAND = 64


def draw_variable_group_index(key, part):
    base_key = jax.random.fold_in(key, 7)
    first_key, second_key = jax.random.split(base_key)
    groups_drawn = jax.random.randint(first_key, (VARS,), 0, G, dtype=jnp.int32)
    order = jax.random.permutation(second_key, VARS)
    forced = groups_drawn.at[order[:G]].set(jnp.arange(G, dtype=jnp.int32))
    return forced.astype(jnp.int32)


def steps_of(rng, extent, cuts, least, high):
    level = 1.0
    for axis_at, parts in cuts:
        steps = jax.random.uniform(jax.random.fold_in(jax.random.fold_in(rng, 6), axis_at), (parts,), jnp.float32, least / len(cuts), high / len(cuts))
        level = level * jnp.repeat(jnp.exp(steps), extent[axis_at] // parts).reshape((-1,) + (1,) * (len(extent) - 1 - axis_at))
    return level


def bell_draw(stream_key, dims, scale, bound, cuts=(), kind=jnp.bfloat16):
    values = jax.random.normal(stream_key, dims, jnp.float32) * scale
    if len(cuts) > 0:
        values = steps_of(stream_key, dims, cuts, -0.22, 0.18) * values
    return jnp.clip(values, min=-bound, max=bound).astype(kind)


def setup_inputs(seed: int = 0) -> dict:
    arg_keys = jax.random.split(jax.random.key(seed), 10)
    return {
        "patches": bell_draw(arg_keys[0], (NS, LEV, LEVEL_CHANNELS, LAT, COLS), 1.0, 6.0, ((0, 4), (3, 64))),
        "variable_group_index": draw_variable_group_index(jax.random.fold_in(arg_keys[9], 71), 0),
        "frozen_patch_weight": bell_draw(arg_keys[2], (G, PIX, EMBED_WIDTH), LEVEL_CHANNELS ** -0.5, 0.625),
        "adapter_down": bell_draw(arg_keys[3], (LEVEL_CHANNELS, ADAPTER_RANK), LEVEL_CHANNELS ** -0.5, 0.625, ((0, 4),)),
        "adapter_up": bell_draw(arg_keys[4], (ADAPTER_RANK, EMBED_WIDTH), ADAPTER_RANK ** -0.5, 1.5, ((1, 4),)),
        "level_merge_weight": bell_draw(arg_keys[5], (LEV, EMBED_WIDTH, EMBED_WIDTH), (LEV * EMBED_WIDTH) ** -0.5, 0.125),
        "window_patch_mixer": bell_draw(arg_keys[6], (WT, WT), WT ** -0.5, 0.625),
        "column_block_owner": jax.random.permutation(arg_keys[7], BLOCKS).astype(jnp.int32),
        "mixed_token_gradient": bell_draw(arg_keys[8], (NS, BLOCKS, LAT, BW, EMBED_WIDTH), ((NS * LAT * COLS * LEV) ** -0.5), 0.01171875, ((0, 4), (1, 64))),
    }


def gelu_exact(values):
    return jax.nn.gelu(values, approximate=False)

def reference(patches, variable_group_index, frozen_patch_weight, adapter_down, adapter_up, level_merge_weight, window_patch_mixer, column_block_owner, mixed_token_gradient):
    selector = (variable_group_index[:, None] == jnp.arange(G, dtype=jnp.int32)[None, :]).astype(jnp.float32)
    base_rows = jnp.einsum('vg,gad->vad', selector, frozen_patch_weight.astype(jnp.float32)).reshape(VARS * PIX, EMBED_WIDTH)
    rank_update = jnp.dot(adapter_down, adapter_up, preferred_element_type=jnp.float32)
    merged = (base_rows + rank_update).astype(jnp.bfloat16)
    merged_f = merged.astype(jnp.float32)
    level_f = level_merge_weight.astype(jnp.float32)
    mix_table = window_patch_mixer.astype(jnp.float32).reshape(WLAT, WLON, WLAT, WLON)
    index_row = jnp.arange(N_BAND, dtype=jnp.int32)
    inverse = lax.optimization_barrier(jnp.sum(jnp.where(column_block_owner[None, :] == index_row[:, None], index_row[None, :], 0), axis=1)).astype(jnp.int32)
    block_width = COLS // N_BAND

    def row_tokens(row_patches):
        embedded = jnp.einsum('lkc,kd->lcd', row_patches.astype(jnp.float32), merged_f).astype(jnp.bfloat16)
        return jnp.einsum('lcd,lde->ce', embedded.astype(jnp.float32), level_f).astype(jnp.bfloat16)

    def row_grad(running, row_inputs):
        row_patches, row_grad_tokens = row_inputs
        grad_embed = jnp.einsum('ce,lde->lcd', row_grad_tokens.astype(jnp.float32), level_f).astype(jnp.bfloat16)
        update = jnp.einsum('lkc,lcd->kd', row_patches.astype(jnp.float32), grad_embed.astype(jnp.float32))
        return (running + update, None)

    def one_sample(inputs):
        sample_patches, sample_grad = inputs
        by_rows = jnp.moveaxis(sample_patches, 2, 0)
        tokens = lax.map(row_tokens, by_rows)
        window_tiles = tokens.astype(jnp.float32).reshape(LAT // WLAT, WLAT, COLS // WLON, WLON, EMBED_WIDTH)
        pre_act = jnp.einsum('iwjv,ajbvd->aibwd', mix_table, window_tiles).reshape(LAT, COLS, EMBED_WIDTH)
        mixed_full = (tokens.astype(jnp.float32) + gelu_exact(pre_act)).astype(jnp.bfloat16)
        mixed_blocks = jnp.moveaxis(jnp.take(mixed_full.reshape(LAT, N_BAND, block_width, EMBED_WIDTH), inverse, axis=1), 1, 0)
        grad_full = jnp.moveaxis(jnp.take(sample_grad, column_block_owner, axis=0), 0, 1).reshape(LAT, COLS, EMBED_WIDTH).astype(jnp.float32)
        grad_pre = jax.vjp(gelu_exact, pre_act)[1](grad_full)[0].astype(jnp.bfloat16)
        grad_tiles = grad_pre.astype(jnp.float32).reshape(LAT // WLAT, WLAT, COLS // WLON, WLON, EMBED_WIDTH)
        spread = jnp.einsum('iwjv,aibwd->ajbvd', mix_table, grad_tiles).reshape(LAT, COLS, EMBED_WIDTH)
        grad_tokens = (grad_full + spread).astype(jnp.bfloat16)
        adapter_weight_gradient, unused_out = lax.scan(row_grad, jnp.zeros((VARS * PIX, EMBED_WIDTH), jnp.float32), (by_rows, grad_tokens))
        return (mixed_blocks, adapter_weight_gradient)
    mixed_all, weight_grads = lax.map(one_sample, (patches, mixed_token_gradient))
    adapter_weight_gradient = lax.optimization_barrier(jnp.sum(weight_grads, axis=0))
    first_factor_gradient = jnp.dot(adapter_weight_gradient, adapter_up.astype(jnp.float32).T, precision=lax.Precision.HIGHEST)
    second_factor_gradient = jnp.dot(adapter_down.astype(jnp.float32).T, adapter_weight_gradient, precision=lax.Precision.HIGHEST)
    return (mixed_all, first_factor_gradient, second_factor_gradient)
```

```python
import jax
import jax.numpy as jnp
import numpy as np
from jax import lax
from jax.experimental import pallas as pl
from jax.experimental.pallas import tpu as pltpu
from jax.sharding import PartitionSpec as P

WLAT = 8
WLON = 12
MESH = pl.DeviceIdType.MESH
F32 = jnp.float32
BF16 = jnp.bfloat16
NT = (((1,), (1,)), ((), ()))
TN = (((0,), (0,)), ((), ()))
CHUNK = 16


def dot(a, b, dims=(((1,), (0,)), ((), ()))):
    return lax.dot_general(a, b, dims, preferred_element_type=F32)


ROWS = [(0, w) for w in range(8)] + [(1, w) for w in range(8)]
ROWS += [(0, w) for w in range(8, 12)] + [(1, w) for w in range(8, 12)]


def window_constants():
    pick = np.zeros((192, 96), np.float32)
    sample = np.zeros((192,), np.int32)
    for r in range(8):
        for u, (n, w) in enumerate(ROWS):
            pick[r * 24 + u, r * 12 + w] = 1
            sample[r * 24 + u] = n
    same = (sample[:, None] == sample[None, :]).astype(np.float32)
    return jnp.asarray(pick, BF16), jnp.asarray(same, F32)


def kernel(
    patches, vgi, frozen, down_t, up, level_w, mixer, owner, grad, pick, same,
    mixed, first_t, second,
    px, px2, wv, gv, send, recv, merge_m, mix_f, mix_b, down_all, up_all,
    pre_v, tok_v, gd_v, gp_v, pk_v, mo, xacc, xb, st1, rb1, st2, rb2, rb3,
    in_sem, send_sem, recv_sem, ad_send, ad_recv, out_sem, red_send, red_recv,
):
    me = lax.axis_index("band")
    rep = lax.axis_index("rep")
    group = me // 8

    load_p = pltpu.make_async_copy(patches, px, in_sem.at[0])
    load_w = pltpu.make_async_copy(level_w, wv, in_sem.at[1])
    load_g = pltpu.make_async_copy(grad, gv, in_sem.at[2])
    load_p.start()
    load_w.start()
    load_g.start()

    barrier = pltpu.get_barrier_semaphore()

    def greet(e, _):
        pl.semaphore_signal(barrier, inc=1, device_id={"band": me ^ e}, device_id_type=MESH)
        return 0

    lax.fori_loop(1, 64, greet, 0)
    for i in range(1, 4):
        pl.semaphore_signal(
            barrier, inc=1, device_id={"rep": lax.rem(rep + i, 4)}, device_id_type=MESH
        )

    down_all[rep] = jnp.zeros((16, 128), BF16)
    down_all[rep, :, 0:20] = down_t[...]
    up_all[rep] = up[...]

    jj = lax.broadcasted_iota(jnp.int32, (64, 768), 0)
    tt = lax.broadcasted_iota(jnp.int32, (64, 768), 1)
    block_of = jnp.where((tt >= jj * 12) & (tt < jj * 12 + 12), 1.0, 0.0).astype(BF16)
    own8 = jnp.broadcast_to(owner[...].astype(F32), (8, 64)).astype(BF16)
    num8 = lax.broadcasted_iota(jnp.int32, (8, 64), 1).astype(F32).astype(BF16)
    t8 = lax.broadcasted_iota(jnp.int32, (8, 768), 1).astype(F32)
    key = dot(own8, block_of) * 16.0 + t8 - 12.0 * dot(num8, block_of)
    key = key.astype(jnp.int32)[0:1, :]

    load_p.wait()
    px2[0:64, :] = px[0, 256:320, :]
    px2[64:128, :] = px[1, 256:320, :]

    pl.semaphore_wait(barrier, 66)

    def adapters(i):
        peer = {"rep": lax.rem(rep + i, 4)}
        return (
            pltpu.make_async_remote_copy(
                down_all.at[rep], down_all.at[rep], ad_send.at[0], ad_recv.at[0],
                device_id=peer, device_id_type=MESH,
            ),
            pltpu.make_async_remote_copy(
                up_all.at[rep], up_all.at[rep], ad_send.at[1], ad_recv.at[1],
                device_id=peer, device_id_type=MESH,
            ),
        )

    for i in range(1, 4):
        for copy in adapters(i):
            copy.start()

    def pack(c, _):
        row = lax.broadcasted_iota(jnp.int32, (CHUNK * 16, 768), 0)
        rr = row & 15
        slot = c * CHUNK + lax.shift_right_logical(row, 4)
        want = (slot ^ me) * 16 + jnp.where(rr < 12, rr, rr - 4)
        z = jnp.where(want == key, 1.0, 0.0).astype(BF16)
        d0 = dot(z, px[0, 0:256, :], NT).reshape(CHUNK, 16, 256)
        d1 = dot(z, px[1, 0:256, :], NT).reshape(CHUNK, 16, 256)
        d2 = dot(z, px2[...], NT).reshape(CHUNK, 16, 128)
        low = lax.broadcasted_iota(jnp.int32, (CHUNK, 8, 256), 1) < 4
        parts = [
            d0[:, 0:8],
            d1[:, 0:8],
            jnp.where(low, d0[:, 8:16], d1[:, 8:16]),
            jnp.concatenate([d2[:, 0:8], d2[:, 8:16]], axis=2),
        ]
        send[pl.ds(c * CHUNK, CHUNK)] = jnp.concatenate(parts, axis=1).astype(BF16)

        def ship(i, _):
            e = c * CHUNK + i

            @pl.when(e != 0)
            def _():
                pltpu.make_async_remote_copy(
                    send.at[e], recv.at[me], send_sem, recv_sem.at[group],
                    device_id={"band": me ^ e}, device_id_type=MESH,
                ).start()

            @pl.when(e == 0)
            def _():
                pltpu.make_async_copy(send.at[0], recv.at[me], recv_sem.at[group]).start()

            return 0

        lax.fori_loop(0, CHUNK, ship, 0)
        return 0

    lax.fori_loop(0, 64 // CHUNK, pack, 0)

    pltpu.make_async_copy(down_all.at[0:3], down_all.at[0:3], ad_recv.at[0]).wait()
    pltpu.make_async_copy(up_all.at[0:3], up_all.at[0:3], ad_recv.at[1]).wait()
    down_f = down_all[0].astype(F32)
    for i in range(1, 4):
        down_f += pltpu.roll(down_all[i].astype(F32), 20 * i, 1)
    down_b = down_f.astype(BF16)
    up_b = jnp.concatenate([up_all[i] for i in range(4)], axis=1)
    base = jnp.concatenate([frozen[vgi[v]].astype(F32) for v in range(5)], axis=0)
    merged = (base + dot(down_b, up_b, TN)[0:80]).astype(BF16)
    load_w.wait()
    for l in range(4):
        merge_m[80 * l : 80 * l + 80, :] = dot(merged, wv[l]).astype(BF16)
    merge_m[320:384, :] = merge_m[256:320, :]

    half = dot(pick[...], mixer[...]).astype(BF16)
    mix_f[...] = (dot(half, pick[...], NT) * same[...]).astype(BF16)
    half_t = dot(pick[...], mixer[...], (((1,), (1,)), ((), ()))).astype(BF16)
    mix_b[...] = (dot(half_t, pick[...], NT) * same[...]).astype(BF16)

    xacc[...] = jnp.zeros((384, 512), F32)
    load_g.wait()

    def out_copy(step, a):
        slot = step & 1
        return pltpu.make_async_copy(
            mo.at[slot], mixed.at[:, pl.ds(a * 8, 8)], out_sem.at[slot]
        )

    def windows(step, _):
        a = group ^ step
        here = recv.at[pl.ds(a * 8, 8)]
        pltpu.make_async_copy(here, here, recv_sem.at[a]).wait()

        @pl.when(step >= 2)
        def _():
            out_copy(step, a).wait()

        got = recv[pl.ds(a * 8, 8)].astype(F32)
        pk_v[:, 0:256] = got[:, 0:24].reshape(192, 256).astype(BF16)
        left = lax.broadcasted_iota(jnp.int32, (8, 8, 128), 2) < 64
        up4 = lax.broadcasted_iota(jnp.int32, (8, 8, 128), 1) < 4
        t0, t1 = got[:, 24:32, 0:128], got[:, 24:32, 128:256]
        zero = jnp.zeros((8, 8, 128), F32)
        tail = jnp.concatenate(
            [
                jnp.where(left, t0, zero),
                jnp.where(left, zero, t0),
                jnp.where(left == up4, t1, zero),
            ],
            axis=1,
        )
        pk_v[:, 256:384] = tail.reshape(192, 128).astype(BF16)
        tok = dot(pk_v[...], merge_m[...]).astype(BF16)
        tok_v[...] = tok.astype(F32)
        pre_v[...] = dot(mix_f[...], tok)

        slot = step & 1
        for i in range(4):
            g0 = gv[0, pl.ds(a * 8 + 2 * i, 2)].astype(F32)
            g1 = gv[1, pl.ds(a * 8 + 2 * i, 2)].astype(F32)
            g = jnp.concatenate(
                [g0[:, 0:8], g1[:, 0:8], g0[:, 8:12], g1[:, 8:12]], axis=1
            ).reshape(48, 512)
            x = pre_v[48 * i : 48 * i + 48, :]
            cdf = 0.5 * (1.0 + lax.erf(x * np.float32(2**-0.5)))
            pdf = jnp.exp(-0.5 * x * x) * np.float32((2 * np.pi) ** -0.5)
            m = (tok_v[48 * i : 48 * i + 48, :] + x * cdf).reshape(2, 24, 512)
            gd_v[48 * i : 48 * i + 48, :] = g
            gp_v[48 * i : 48 * i + 48, :] = (g * (cdf + x * pdf)).astype(BF16)
            m0 = jnp.concatenate([m[:, 0:8], m[:, 16:20]], axis=1)
            m1 = jnp.concatenate([m[:, 8:16], m[:, 20:24]], axis=1)
            mo[slot, 0, 2 * i : 2 * i + 2] = m0.astype(BF16)
            mo[slot, 1, 2 * i : 2 * i + 2] = m1.astype(BF16)
        out_copy(step, a).start()
        grad_tok = (gd_v[...] + dot(mix_b[...], gp_v[...])).astype(BF16)
        xacc[...] += dot(pk_v[...], grad_tok, TN)
        return 0

    lax.fori_loop(0, 8, windows, 0)

    xb[0:256, :] = xacc[0:256, :].astype(BF16)
    xb[256:320, :] = (xacc[256:320, :] + xacc[320:384, :]).astype(BF16)
    wg = dot(xb[0:80, :], wv[0], NT)
    for l in range(1, 4):
        wg += dot(xb[80 * l : 80 * l + 80, :], wv[l], NT)
    wgb = wg.astype(BF16)
    sec = dot(down_b[:, 0:80], wgb)
    fst = dot(up_b, wgb, NT)
    for i in range(4):
        st1[i, 0:16, :] = sec[:, 128 * i : 128 * i + 128]
        st1[i, 16:32, :] = jnp.zeros((16, 128), F32)
        st1[i, 16:32, 0:80] = fst

    z = lax.rem(me // 2, 8)
    xc = (me // 16) * 2 + lax.rem(me, 2)

    rb1[rep] = st1[rep]
    for i in range(1, 4):
        to = lax.rem(rep + i, 4)
        pltpu.make_async_remote_copy(
            st1.at[to], rb1.at[rep], red_send.at[0], red_recv.at[0],
            device_id={"rep": to}, device_id_type=MESH,
        ).start()
    pltpu.make_async_copy(rb1.at[0:3], rb1.at[0:3], red_recv.at[0]).wait()
    st2[0] = rb1[0] + rb1[1] + rb1[2] + rb1[3]

    rb2[xc] = st2[0]
    for j in range(1, 8):
        to = xc ^ j
        pltpu.make_async_remote_copy(
            st2.at[0], rb2.at[xc], red_send.at[1], red_recv.at[1],
            device_id={"band": (to // 2) * 16 + z * 2 + lax.rem(to, 2)}, device_id_type=MESH,
        ).start()
    pltpu.make_async_copy(rb2.at[0:7], rb2.at[0:7], red_recv.at[1]).wait()
    total = rb2[0]
    for j in range(1, 8):
        total += rb2[j]
    st2[1] = total

    rb3[z] = st2[1]
    for j in range(1, 8):
        to = z ^ j
        pltpu.make_async_remote_copy(
            st2.at[1], rb3.at[z], red_send.at[2], red_recv.at[2],
            device_id={"band": (me // 16) * 16 + to * 2 + lax.rem(me, 2)}, device_id_type=MESH,
        ).start()
    pltpu.make_async_copy(rb3.at[0:7], rb3.at[0:7], red_recv.at[2]).wait()
    total = rb3[0]
    for j in range(1, 8):
        total += rb3[j]
    second[...] = total[0:16]
    first_t[...] = pltpu.roll(total[16:32], lax.rem(128 - 20 * rep, 128), 1)[:, 0:20]

    out_copy(6, group).wait()
    out_copy(7, group).wait()
    pltpu.make_async_copy(send.at[1:64], send.at[1:64], send_sem).wait()
    pltpu.make_async_copy(down_all.at[0:3], down_all.at[0:3], ad_send.at[0]).wait()
    pltpu.make_async_copy(up_all.at[0:3], up_all.at[0:3], ad_send.at[1]).wait()
    pltpu.make_async_copy(rb1.at[0:3], rb1.at[0:3], red_send.at[0]).wait()
    pltpu.make_async_copy(rb2.at[0:7], rb2.at[0:7], red_send.at[1]).wait()
    pltpu.make_async_copy(rb3.at[0:7], rb3.at[0:7], red_send.at[2]).wait()


def on_device(
    patches,
    variable_group_index,
    frozen_patch_weight,
    adapter_down,
    adapter_up,
    level_merge_weight,
    window_patch_mixer,
    column_block_owner,
    mixed_token_gradient,
):
    pick, same = window_constants()
    vmem = pl.BlockSpec(memory_space=pltpu.VMEM)
    smem = pl.BlockSpec(memory_space=pltpu.SMEM)
    hbm = pl.BlockSpec(memory_space=pl.ANY)
    dma = pltpu.SemaphoreType.DMA
    mixed, first_t, second = pl.pallas_call(
        kernel,
        out_shape=(
            jax.ShapeDtypeStruct((2, 64, 12, 512), BF16),
            jax.ShapeDtypeStruct((16, 20), F32),
            jax.ShapeDtypeStruct((16, 128), F32),
        ),
        in_specs=[hbm, smem, vmem, vmem, vmem, hbm, vmem, vmem, hbm, vmem, vmem],
        out_specs=(hbm, vmem, vmem),
        scratch_shapes=[
            pltpu.VMEM((2, 320, 768), BF16),
            pltpu.VMEM((128, 768), BF16),
            pltpu.VMEM((4, 512, 512), BF16),
            pltpu.VMEM((2, 64, 12, 512), BF16),
            pltpu.VMEM((64, 32, 256), BF16),
            pltpu.VMEM((64, 32, 256), BF16),
            pltpu.VMEM((384, 512), BF16),
            pltpu.VMEM((192, 192), BF16),
            pltpu.VMEM((192, 192), BF16),
            pltpu.VMEM((4, 16, 128), BF16),
            pltpu.VMEM((4, 16, 128), BF16),
            pltpu.VMEM((192, 512), F32),
            pltpu.VMEM((192, 512), F32),
            pltpu.VMEM((192, 512), F32),
            pltpu.VMEM((192, 512), BF16),
            pltpu.VMEM((192, 384), BF16),
            pltpu.VMEM((2, 2, 8, 12, 512), BF16),
            pltpu.VMEM((384, 512), F32),
            pltpu.VMEM((320, 512), BF16),
            pltpu.VMEM((4, 32, 128), F32),
            pltpu.VMEM((4, 32, 128), F32),
            pltpu.VMEM((2, 32, 128), F32),
            pltpu.VMEM((8, 32, 128), F32),
            pltpu.VMEM((8, 32, 128), F32),
            dma((3,)),
            dma,
            dma((8,)),
            dma((2,)),
            dma((2,)),
            dma((2,)),
            dma((3,)),
            dma((3,)),
        ],
        compiler_params=pltpu.CompilerParams(
            collective_id=0, has_side_effects=True, vmem_limit_bytes=48 << 20
        ),
        name="patch_window_kernel",
    )(
        patches.reshape(2, 320, 768),
        variable_group_index,
        frozen_patch_weight,
        adapter_down.T,
        adapter_up,
        level_merge_weight,
        window_patch_mixer,
        column_block_owner.reshape(1, 64),
        mixed_token_gradient.reshape(2, 64, 12, 512),
        pick,
        same,
    )
    return (mixed.reshape(2, 1, 64, 12, 512), first_t.T, second)


def solution(mesh):
    in_specs = (
        P("rep", None, None, "band", None),
        P(),
        P(),
        P("rep", None),
        P(None, "rep"),
        P(),
        P(),
        P(),
        P("rep", "band", None, None, None),
    )
    out_specs = (P("rep", "band", None, None, None), P("rep", None), P(None, "rep"))
    return jax.shard_map(
        on_device, mesh=mesh, in_specs=in_specs, out_specs=out_specs, check_vma=False
    )
```
